256 devices in a mesh: grp: 8 (over y, core), dev: 32 (over z, x).
Axes of the slice: x: 4, y: 4, z: 8, core: 2. Of those that a mesh axis runs over, the one named last changes fastest.
Arguments:
- charges: bfloat16 [8192, 16, 128], P(('grp', 'dev')), may hold values from -6 to 6
- leaf_basis: bfloat16 [8192, 128, 64], P(('grp', 'dev')), may hold values from -0.5 to 0.5
- near_blocks: bfloat16 [40960, 128, 128], P(('grp', 'dev')), may hold values from -0.375 to 0.375
- near_target: int32 [40960], P(('grp', 'dev')), may hold values from 0 to 8191, as said below
- near_source: int32 [40960], P(('grp', 'dev')), may hold values from 0 to 8191, as said below
- near_count: int32 [256], P(('grp', 'dev')), may hold values from 40 to 160, as said below
- leaf_far: int32 [8192, 16], P(('grp', 'dev')), may hold values from 0 to 8191, as said below
- leaf_far_couple: int32 [8192, 16], P(('grp', 'dev')), may hold values from 0 to 315
- leaf_trans: int32 [8192], P(('grp', 'dev')), may hold values from 0 to 7
- dev_trans: int32 [256], P(('grp', 'dev')), may hold values from 0 to 7
- dev_list: int32 [256, 4], P(('grp', 'dev')), may hold values from 0 to 255, as said below
- dev_couple: int32 [256, 4], P(('grp', 'dev')), may hold values from 0 to 315
- grp_couple: int32 [8, 8], replicated, may hold values from 0 to 315
- trans_leaf: float32 [8, 64, 64], replicated, may hold values from -0.375 to 0.375
- trans_dev: float32 [8, 64, 64], replicated, may hold values from -0.25 to 0.25
- couple_table: float32 [316, 64, 64], replicated, may hold values from -0.375 to 0.375
Outputs:
- potentials: float32 [8192, 16, 128], P(('grp', 'dev'))
The draws below stay inside these ranges and needn't reach their ends.
Inputs may be any that keep to these rules, and one draw needn't show every extreme that they name: `near_count`: live slots of a device are at least a quarter of its 160; some device has all slots live and some device exactly 40. `near_target`: slot s names a leaf of device s // 160. `near_source`: slot s names a leaf within 16 leaves of device s // 160's range of leaves; on every device both ends of that window are named where they exist. `leaf_far`: leaf b names leaves within 16 leaves of the range of its device; on every device both ends of that window are named where they exist. `dev_list`: box d names boxes of its own subtree, never itself nor the two next to it in cyclic order within the subtree.
All inputs are finite; a program needn't handle non-finite values.
Results may differ from the reference program's by a relative error of at most 0.0024.
Values may be sent and summed in bfloat16 or wider, within the bound.
A program may use at most 128 MiB of HBM per device.

```python
import jax
import jax.numpy as jnp
from jax import lax

R = 16
P_SIZE = 128
K = 64
NTRANS = 8
NCOUPLE = 316
NFAR = 16
NL1 = 4
LEAF_DEV = 32
NB_DEV = 160
HALO = 16
GROUPS = 8
GDEV = 32
BOXES = 256
NLEAF = 8192


def window_sources(key, rows, per_row, per_device):
    device_of = (jnp.arange(rows) // per_device).astype(jnp.int32)
    lowest = device_of * LEAF_DEV - HALO
    highest = device_of * LEAF_DEV + LEAF_DEV + HALO - 1
    offsets = jax.random.randint(key, (rows, per_row), 0, LEAF_DEV + 2 * HALO)
    values = lowest[:, None] + offsets
    row_local = (jnp.arange(rows) % per_device)[:, None]
    column = jnp.arange(per_row)[None, :]
    return (values, lowest, highest, row_local, column)


def draw_near_count(key, part):
    first_key, second_key, third_key = jax.random.split(jax.random.fold_in(key, 11), 3)
    counts = NB_DEV // 4 + jax.random.randint(first_key, (BOXES,), 0, NB_DEV - NB_DEV // 4 + 1)
    busiest = jax.random.randint(second_key, (), 0, BOXES)
    lightest = (busiest + 1 + jax.random.randint(third_key, (), 0, BOXES - 1)) % BOXES
    counts = counts.at[busiest].set(NB_DEV)
    counts = counts.at[lightest].set(NB_DEV // 4)
    return counts.astype(jnp.int32)


def draw_near_target(key, part):
    slots = BOXES * NB_DEV
    device_of = (jnp.arange(slots) // NB_DEV).astype(jnp.int32)
    offsets = jax.random.randint(jax.random.fold_in(key, 12), (slots,), 0, LEAF_DEV)
    local_slot = jnp.arange(slots) % NB_DEV
    offsets = jnp.where(local_slot == 0, 0, jnp.where(local_slot == 1, LEAF_DEV - 1, offsets))
    return (device_of * LEAF_DEV + offsets).astype(jnp.int32)


def draw_near_source(key, part):
    slots = BOXES * NB_DEV
    values, lowest, highest, row_local, column = window_sources(jax.random.fold_in(key, 13), slots, 1, NB_DEV)
    values = values[:, 0]
    values = jnp.where(row_local[:, 0] == 0, lowest, jnp.where(row_local[:, 0] == 1, highest, values))
    return jnp.clip(values, 0, NLEAF - 1).astype(jnp.int32)


def draw_leaf_far(key, part):
    values, lowest, highest, row_local, column = window_sources(jax.random.fold_in(key, 14), NLEAF, NFAR, LEAF_DEV)
    values = jnp.where((row_local == 0) & (column == 0), lowest[:, None], values)
    values = jnp.where((row_local == LEAF_DEV - 1) & (column == NFAR - 1), highest[:, None], values)
    return jnp.clip(values, 0, NLEAF - 1).astype(jnp.int32)


def draw_dev_list(key, part):
    box_ids = jnp.arange(BOXES).astype(jnp.int32)
    subtree = box_ids // GDEV
    member = box_ids % GDEV
    offsets = jax.random.randint(jax.random.fold_in(key, 15), (BOXES, NL1), 0, GDEV - 3)
    chosen = (member[:, None] + 2 + offsets) % GDEV
    return (subtree[:, None] * GDEV + chosen).astype(jnp.int32)


def touch_ends(entries, stream_key, smallest, top_value):
    dims = entries.shape
    index_at = [jax.random.randint(jax.random.fold_in(stream_key, axis), (), 0, dims[axis]) for axis in range(len(dims))]
    entries = entries.at[tuple(index_at)].set(smallest)
    longest = dims.index(max(dims))
    index_at[longest] = (index_at[longest] + 1) % dims[longest]
    return entries.at[tuple(index_at)].set(top_value)


def block_levels(rng, dims, shards, smallest, top_value):
    loudness, own = 1.0, jax.random.fold_in(rng, 6)
    for position, shards_of in shards:
        draws = jnp.exp(jax.random.uniform(jax.random.fold_in(own, position), (shards_of,), jnp.float32, smallest / len(shards), top_value / len(shards)))
        loudness = loudness * jnp.repeat(draws, dims[position] // shards_of).reshape([-1 if axis == position else 1 for axis in range(len(dims))])
    return loudness


def bell_draw(stream_key, shape, width, bound, pieces=(), kind=jnp.bfloat16):
    gain = block_levels(stream_key, shape, pieces, -0.22, 0.18) if pieces else 1.0
    entries = jax.random.normal(stream_key, shape, jnp.float32) * width * gain
    return jnp.minimum(jnp.maximum(entries, -bound), bound).astype(kind)


def setup_inputs(seed: int = 0) -> dict:
    streams_of = jax.random.split(jax.random.key(seed), 17)
    return {
        "charges": bell_draw(streams_of[0], (NLEAF, R, P_SIZE), 1.0, 6.0, ((0, 256),)),
        "leaf_basis": bell_draw(streams_of[1], (NLEAF, P_SIZE, K), P_SIZE ** -0.5, 0.5, ((0, 256),)),
        "near_blocks": bell_draw(streams_of[2], (BOXES * NB_DEV, P_SIZE, P_SIZE), (2 * P_SIZE) ** -0.5, 0.375, ((0, 256),)),
        "near_target": draw_near_target(jax.random.fold_in(streams_of[16], 71), 0),
        "near_source": draw_near_source(jax.random.fold_in(streams_of[16], 71), 0),
        "near_count": draw_near_count(jax.random.fold_in(streams_of[16], 71), 0),
        "leaf_far": draw_leaf_far(jax.random.fold_in(streams_of[16], 71), 0),
        "leaf_far_couple": touch_ends(jax.random.randint(streams_of[7], (NLEAF, NFAR), 0, NCOUPLE), jax.random.fold_in(streams_of[7], 1), 0, NCOUPLE - 1).astype(jnp.int32),
        "leaf_trans": touch_ends(jax.random.randint(streams_of[8], (NLEAF,), 0, NTRANS), jax.random.fold_in(streams_of[8], 1), 0, NTRANS - 1).astype(jnp.int32),
        "dev_trans": touch_ends(jax.random.randint(streams_of[9], (BOXES,), 0, NTRANS), jax.random.fold_in(streams_of[9], 1), 0, NTRANS - 1).astype(jnp.int32),
        "dev_list": draw_dev_list(jax.random.fold_in(streams_of[16], 71), 0),
        "dev_couple": touch_ends(jax.random.randint(streams_of[11], (BOXES, NL1), 0, NCOUPLE), jax.random.fold_in(streams_of[11], 1), 0, NCOUPLE - 1).astype(jnp.int32),
        "grp_couple": touch_ends(jax.random.randint(streams_of[12], (GROUPS, GROUPS), 0, NCOUPLE), jax.random.fold_in(streams_of[12], 1), 0, NCOUPLE - 1).astype(jnp.int32),
        "trans_leaf": bell_draw(streams_of[13], (NTRANS, K, K), (4 * K) ** -0.5, 0.375, (), jnp.float32),
        "trans_dev": bell_draw(streams_of[14], (NTRANS, K, K), (8 * K) ** -0.5, 0.25, (), jnp.float32),
        "couple_table": bell_draw(streams_of[15], (NCOUPLE, K, K), (4 * K) ** -0.5, 0.375, (), jnp.float32),
    }


HIGHEST = lax.Precision.HIGHEST


def reference(charges, leaf_basis, near_blocks, near_target, near_source, near_count, leaf_far, leaf_far_couple, leaf_trans, dev_trans, dev_list, dev_couple, grp_couple, trans_leaf, trans_dev, couple_table):
    f32 = jnp.float32
    basis_wide = leaf_basis.astype(f32)
    leaf_moment = jnp.einsum('lrp,lpk->lrk', charges.astype(f32), basis_wide, precision=HIGHEST)
    child_maps = trans_leaf[leaf_trans].reshape(BOXES, LEAF_DEV, K, K)
    box_moment = jnp.einsum('blrk,blkj->brj', leaf_moment.reshape(BOXES, LEAF_DEV, R, K), child_maps, precision=HIGHEST)
    up_maps = trans_dev[dev_trans]
    group_moment = jnp.einsum('gdrk,gdkj->grj', box_moment.reshape(GROUPS, GDEV, R, K), up_maps.reshape(GROUPS, GDEV, K, K), precision=HIGHEST)
    away = 1.0 - jnp.eye(GROUPS, dtype=f32)
    group_local = jnp.einsum('gh,hrk,ghkj->grj', away, group_moment, couple_table[grp_couple], precision=HIGHEST)
    owner_group = jnp.arange(BOXES) // GDEV
    box_local = jnp.einsum('brj,bkj->brk', group_local[owner_group], up_maps, precision=HIGHEST)
    box_local = box_local + jnp.einsum('bnrk,bnkj->brj', box_moment[dev_list], couple_table[dev_couple], precision=HIGHEST)
    leaf_local = jnp.einsum('brj,blkj->blrk', box_local, child_maps, precision=HIGHEST).reshape(NLEAF, R, K)

    def far_box(inputs):
        sources, kinds = inputs
        return jnp.einsum('lfrk,lfkj->lrj', leaf_moment[sources], couple_table[kinds], precision=HIGHEST)

    far_terms = lax.map(far_box, (leaf_far.reshape(BOXES, LEAF_DEV, NFAR), leaf_far_couple.reshape(BOXES, LEAF_DEV, NFAR)))
    leaf_local = (leaf_local + far_terms.reshape(NLEAF, R, K)).astype(jnp.bfloat16)
    far_part = jnp.einsum('lrk,lpk->lrp', leaf_local.astype(f32), basis_wide, precision=HIGHEST)

    def near_box(inputs):
        blocks, targets, sources, count, box_index = inputs
        picked = charges[sources].astype(f32)
        product = jnp.einsum('sij,srj->sri', blocks.astype(f32), picked, precision=HIGHEST)
        live = jnp.arange(NB_DEV) < count
        local_target = targets - box_index * LEAF_DEV
        onehot = ((local_target[None, :] == jnp.arange(LEAF_DEV)[:, None]) & live[None, :]).astype(f32)
        return jnp.einsum('ts,sri->tri', onehot, product, precision=HIGHEST)

    near_terms = lax.map(near_box, (near_blocks.reshape(BOXES, NB_DEV, P_SIZE, P_SIZE), near_target.reshape(BOXES, NB_DEV), near_source.reshape(BOXES, NB_DEV), near_count, jnp.arange(BOXES).astype(jnp.int32)))
    return near_terms.reshape(NLEAF, R, P_SIZE) + far_part
```

```python
import functools

import jax
import jax.numpy as jnp
from jax import lax
from jax.experimental import pallas as pl
from jax.experimental.pallas import tpu as pltpu
from jax.sharding import PartitionSpec as P

f32, bf16 = jnp.float32, jnp.bfloat16
MESH = pl.DeviceIdType.MESH
NT = (((1,), (1,)), ((), ()))


def split(x):
    high = x.astype(bf16)
    return high, (x - high.astype(f32)).astype(bf16)


def inside(index, size):
    return lax.min(lax.max(index, 0), size - 1)


def left_half(shape):
    return lax.broadcasted_iota(jnp.int32, shape, 1) < 64


def compact(doubled):
    high, low = split(doubled)
    return jnp.where(left_half(high.shape), high.astype(f32), low.astype(f32)).astype(bf16)


def doubled_sum(total):
    return total + pltpu.roll(total, 64, 1)


def spread_matrix():
    row = lax.broadcasted_iota(jnp.int32, (128, 512), 0)
    column = lax.broadcasted_iota(jnp.int32, (128, 512), 1)
    hit = (row >> 5 == column >> 7) & (row & 31 == column & 31)
    return hit.astype(f32).astype(bf16)


def spread(blocks, matrix):
    wide = jnp.dot(blocks, matrix, preferred_element_type=f32).astype(bf16)
    out = []
    for i in range(blocks.shape[0] // 16):
        rows = wide[i * 16 : (i + 1) * 16]
        out.append(jnp.concatenate([rows[:, g * 128 : (g + 1) * 128] for g in range(4)], axis=0))
    return out


def times_maps(wide, maps):
    weights = []
    for m in maps:
        weights.extend(split(m))
    weights = jnp.concatenate(weights, axis=0)
    if len(wide) == 1:
        lanes = wide[0][:, :64]
    else:
        half = left_half((64, 128))
        lanes = jnp.concatenate(
            [jnp.where(half, wide[i], wide[i + 1]) for i in range(0, len(wide), 2)], axis=1
        )
    return jnp.dot(lanes, weights, preferred_element_type=f32)


def fold(total):
    kept = jnp.where(
        left_half((16, 128)), total[0:16] + total[32:48], total[16:32] + total[48:64]
    )
    return doubled_sum(kept)


def kernel(
    sizes,
    charges,
    basis,
    blocks,
    target,
    source,
    count,
    far,
    far_couple,
    leaf_trans,
    dev_trans,
    dev_list,
    dev_couple,
    grp_couple,
    trans_leaf,
    trans_dev,
    couple,
    out,
    window,
    bt,
    blk,
    tl,
    td,
    raw,
    table,
    small,
    small_t,
    cwin,
    mwin,
    ubuf,
    xbuf,
    zbuf,
    bbuf,
    usend,
    vsend,
    wsend,
    prod,
    nbuf,
    farb,
    ybuf,
    local_sem,
    chunk_sem,
    halo_send,
    halo_recv,
    u_send,
    u_recv,
    x_send,
    x_recv,
    bx_send,
    bx_recv,
    z_send,
    z_recv,
    bz_send,
    bz_recv,
):
    groups, zs, xs = sizes
    per_group = zs * xs
    leaves = out.shape[0]
    margin = leaves // 2
    slots = blk.shape[0]
    types = table.shape[0]
    rows_of = table.reshape(types * 32, 128)
    ntrans = tl.shape[0]
    chunks = 4
    per_chunk = 32 // chunks
    g, d = lax.axis_index("grp"), lax.axis_index("dev")
    z, x = lax.div(d, xs), lax.rem(d, xs)
    me = g * per_group + d
    total = groups * per_group
    right, left = lax.rem(me + 1, total), lax.rem(me + total - 1, total)
    first = me * leaves - margin

    def at(index):
        return {"grp": lax.div(index, per_group), "dev": lax.rem(index, per_group)}

    def group_peer(o):
        return {"grp": lax.rem(g + o, groups), "dev": d}

    def x_peer(o):
        return {"grp": g, "dev": z * xs + lax.rem(x + o, xs)}

    def z_peer(o):
        return {"grp": g, "dev": lax.rem(z + o, zs) * xs + x}

    loads = []
    for i, (a, b) in enumerate(
        (
            (charges, window.at[pl.ds(margin, leaves)]),
            (basis, bt),
            (trans_leaf, tl),
            (trans_dev, td),
        )
    ):
        loads.append(pltpu.make_async_copy(a, b, local_sem.at[i]))
    raw_loads = []
    for c in range(chunks):
        for half in range(2):
            rows = pl.ds(half * 32 + c * per_chunk, per_chunk)
            raw_loads.append(
                pltpu.make_async_copy(couple.at[rows], raw.at[rows], chunk_sem.at[c * 2 + half])
            )
    block_load = pltpu.make_async_copy(blocks, blk, local_sem.at[4])
    for copy in loads + raw_loads + [block_load]:
        copy.start()

    barrier = pltpu.get_barrier_semaphore()
    peers = (
        [at(left), at(right)]
        + [group_peer(o) for o in range(1, groups)]
        + [x_peer(o) for o in range(1, xs)]
        + [z_peer(o) for o in range(1, zs)]
    )
    for peer in peers:
        pl.semaphore_signal(barrier, inc=1, device_id=peer, device_id_type=MESH)

    matrix = spread_matrix()
    loads[2].wait()
    loads[3].wait()
    for i in range(2 * ntrans):
        m = tl[i] if i < ntrans else td[i - ntrans]
        small[i] = jnp.concatenate([m[:32], m[32:]], axis=1)
        small_t[i] = compact(jnp.concatenate([m, m], axis=1))

    loads[0].wait()
    loads[1].wait()

    def moments(step, carry):
        for j in range(8):
            leaf = step * 8 + j
            b = bt[leaf]
            m = lax.dot_general(
                window[margin + leaf],
                jnp.concatenate([b, b], axis=0),
                NT,
                preferred_element_type=f32,
            )
            cwin[margin + leaf] = compact(m)
        return carry

    lax.fori_loop(0, leaves // 8, moments, 0)

    def widen(start):
        def body(step, carry):
            c = jnp.concatenate([cwin[start + step * 8 + j] for j in range(8)], axis=0)
            for j, w in enumerate(spread(c, matrix)):
                mwin[start + step * 8 + j] = w
            return carry

        return body

    lax.fori_loop(0, leaves // 8, widen(margin), 0)

    def small_map(i):
        return small[i]

    def big_map(i):
        return table[i]

    def to_box(step, carry):
        picks = [step * 4 + j for j in range(4)]
        return carry + times_maps(
            [mwin[margin + p] for p in picks], [small_map(leaf_trans[p]) for p in picks]
        )

    box = compact(fold(lax.fori_loop(0, leaves // 4, to_box, jnp.zeros((64, 128), f32))))
    bbuf[d] = box
    dtrans = dev_trans[0]
    usend[...] = compact(fold(times_maps(spread(box, matrix), [small_map(ntrans + dtrans)])))
    ubuf[g] = jnp.zeros((16, 128), bf16)

    pl.semaphore_wait(barrier, len(peers))

    def remote(src, dst, send, recv, i, peer):
        copy = pltpu.make_async_remote_copy(
            src_ref=src,
            dst_ref=dst,
            send_sem=send.at[i],
            recv_sem=recv.at[i],
            device_id=peer,
            device_id_type=MESH,
        )
        copy.start()
        return copy

    to_groups = [
        remote(usend, ubuf.at[g], u_send, u_recv, o - 1, group_peer(o)) for o in range(1, groups)
    ]
    box_x = [
        remote(bbuf.at[d], bbuf.at[d], bx_send, bx_recv, o - 1, x_peer(o))
        for o in range(1, xs)
    ]
    low, high = pl.ds(0, margin), pl.ds(leaves, margin)
    end_low, end_high = pl.ds(margin + leaves, margin), pl.ds(margin, margin)
    charge_halo = [
        remote(charges.at[pl.ds(leaves - margin, margin)], window.at[low], halo_send, halo_recv, 0, at(right)),
        remote(charges.at[pl.ds(0, margin)], window.at[end_low], halo_send, halo_recv, 1, at(left)),
    ]
    moment_halo = [
        remote(cwin.at[high], cwin.at[low], halo_send, halo_recv, 2, at(right)),
        remote(cwin.at[end_high], cwin.at[end_low], halo_send, halo_recv, 3, at(left)),
    ]

    for c in range(chunks):
        raw_loads[2 * c].wait()
        raw_loads[2 * c + 1].wait()

        def turn(i, carry):
            k = c * per_chunk + i
            both = jnp.concatenate([raw[k], raw[k + 32]], axis=0)
            rows_of[pl.ds(k, types, stride=32), :] = both.T
            return carry

        lax.fori_loop(0, per_chunk, turn, 0)

    for copy in to_groups:
        copy.wait_recv()
    share = jnp.zeros((64, 128), f32)
    for h in range(0, groups, 4):
        picks = list(range(h, min(h + 4, groups)))
        rows = jnp.concatenate([ubuf[p] for p in picks], axis=0)
        share = share + times_maps(spread(rows, matrix), [big_map(grp_couple[g, p]) for p in picks])
    vsend[...] = compact(fold(share))
    xbuf[x] = vsend[...]
    share_x = [
        remote(vsend, xbuf.at[x], x_send, x_recv, o - 1, x_peer(o)) for o in range(1, xs)
    ]
    for copy in box_x:
        copy.wait_recv()
    plane = pl.ds(z * xs, xs)
    box_z = [
        remote(bbuf.at[plane], bbuf.at[plane], bz_send, bz_recv, o - 1, z_peer(o)) for o in range(1, zs)
    ]

    for copy in charge_halo:
        copy.wait_recv()
    block_load.wait()

    def near(step, carry):
        for j in range(8):
            s = step * 8 + j
            product = lax.dot_general(
                window[inside(source[s] - first, 2 * leaves)], blk[s], NT, preferred_element_type=f32
            )
            prod[pl.ds(pl.multiple_of(s * 16, 16), 16), :] = product
        return carry

    half_slots = slots // 16
    lax.fori_loop(0, half_slots, near, 0)

    for copy in share_x:
        copy.wait_recv()
    row = xbuf[0].astype(f32)
    for i in range(1, xs):
        row = row + xbuf[i].astype(f32)
    wsend[...] = compact(doubled_sum(row))
    zbuf[z] = wsend[...]
    share_z = [
        remote(wsend, zbuf.at[z], z_send, z_recv, o - 1, z_peer(o)) for o in range(1, zs)
    ]

    lax.fori_loop(half_slots, slots // 8, near, 0)

    live = lax.broadcasted_iota(jnp.int32, (leaves, slots), 1) < count[0]
    which = lax.broadcasted_iota(jnp.int32, (leaves, slots), 0) + me * leaves
    pick = ((which == target[...]) & live).astype(f32).astype(bf16)

    def gather_near(step, carry):
        rows = [prod[pl.ds(step * 2 + j, slots, stride=16), :] for j in range(2)]
        high, low = split(jnp.concatenate(rows, axis=1))
        summed = jnp.dot(pick, high, preferred_element_type=f32) + jnp.dot(
            pick, low, preferred_element_type=f32
        )
        for j in range(2):
            start = pl.multiple_of((step * 2 + j) * leaves, leaves)
            nbuf[pl.ds(start, leaves), :] = summed[:, j * 128 : (j + 1) * 128]
        return carry

    lax.fori_loop(0, 8, gather_near, 0)

    for copy in moment_halo:
        copy.wait_recv()
    lax.fori_loop(0, margin // 8, widen(0), 0)
    lax.fori_loop(0, margin // 8, widen(margin + leaves), 0)

    nfar = far.shape[0]

    def far_field(leaf, carry):
        acc = jnp.zeros((64, 128), f32)
        for f in range(0, nfar, 4):
            acc = acc + times_maps(
                [mwin[inside(far[f + j, leaf] - first, 2 * leaves)] for j in range(4)],
                [big_map(far_couple[f + j, leaf]) for j in range(4)],
            )
        farb[leaf] = fold(acc)[:, :64]
        return carry

    lax.fori_loop(0, leaves, far_field, 0)

    for copy in share_z:
        copy.wait_recv()
    for copy in box_z:
        copy.wait_recv()
    row = zbuf[0].astype(f32)
    for i in range(1, zs):
        row = row + zbuf[i].astype(f32)
    high_g, low_g = split(doubled_sum(row))
    down = lax.dot_general(
        jnp.concatenate([high_g, low_g], axis=0), small_t[ntrans + dtrans], NT, preferred_element_type=f32
    )
    listed = [inside(dev_list[0, n] - g * per_group, per_group) for n in range(4)]
    rows = jnp.concatenate([bbuf[b] for b in listed], axis=0)
    beside = fold(
        times_maps(spread(rows, matrix), [big_map(dev_couple[0, n]) for n in range(4)])
    )
    down = down[:16] + down[16:]
    high_b, low_b = split(jnp.concatenate([down, down], axis=1) + beside)
    both = jnp.concatenate([high_b, low_b], axis=0)
    for t in range(ntrans):
        y = lax.dot_general(both, small_t[t], NT, preferred_element_type=f32)
        ybuf[t] = y[:16] + y[16:]

    def finish(step, carry):
        for j in range(4):
            leaf = step * 4 + j
            rounded = (ybuf[leaf_trans[leaf]] + farb[leaf]).astype(bf16)
            out[leaf] = nbuf[pl.ds(leaf, 16, stride=leaves), :] + jnp.dot(
                rounded, bt[leaf], preferred_element_type=f32
            )
        return carry

    lax.fori_loop(0, leaves // 4, finish, 0)

    for copy in to_groups + box_x + charge_halo + moment_halo + share_x + box_z + share_z:
        copy.wait_send()


def local(
    sizes,
    charges,
    leaf_basis,
    near_blocks,
    near_target,
    near_source,
    near_count,
    leaf_far,
    leaf_far_couple,
    leaf_trans,
    dev_trans,
    dev_list,
    dev_couple,
    grp_couple,
    trans_leaf,
    trans_dev,
    couple_table,
):
    groups, zs, xs = sizes
    leaves, r, panels = charges.shape
    slots = near_blocks.shape[0]
    types, k, _ = couple_table.shape
    ntrans = trans_leaf.shape[0]
    width = 2 * leaves
    hbm = pl.BlockSpec(memory_space=pl.ANY)
    smem = pl.BlockSpec(memory_space=pltpu.SMEM)
    vmem = pl.BlockSpec(memory_space=pltpu.VMEM)
    dma = pltpu.SemaphoreType.DMA
    return pl.pallas_call(
        functools.partial(kernel, sizes),
        out_shape=jax.ShapeDtypeStruct((leaves, r, panels), f32),
        in_specs=[hbm, hbm, hbm, vmem] + [smem] * 9 + [hbm, hbm, hbm],
        out_specs=vmem,
        scratch_shapes=[
            pltpu.VMEM((width, r, panels), bf16),
            pltpu.VMEM((leaves, k, panels), bf16),
            pltpu.VMEM((slots, panels, panels), bf16),
            pltpu.VMEM((ntrans, k, k), f32),
            pltpu.VMEM((ntrans, k, k), f32),
            pltpu.VMEM((k, k, types), f32),
            pltpu.VMEM((types, 32, 128), f32),
            pltpu.VMEM((2 * ntrans, 32, 128), f32),
            pltpu.VMEM((2 * ntrans, k, 128), bf16),
            pltpu.VMEM((width, r, 128), bf16),
            pltpu.VMEM((width, 64, 128), bf16),
            pltpu.VMEM((groups, r, 128), bf16),
            pltpu.VMEM((xs, r, 128), bf16),
            pltpu.VMEM((zs, r, 128), bf16),
            pltpu.VMEM((zs * xs, r, 128), bf16),
            pltpu.VMEM((r, 128), bf16),
            pltpu.VMEM((r, 128), bf16),
            pltpu.VMEM((r, 128), bf16),
            pltpu.VMEM((slots * r, panels), f32),
            pltpu.VMEM((r * leaves, panels), f32),
            pltpu.VMEM((leaves, r, k), f32),
            pltpu.VMEM((ntrans, r, k), f32),
            dma((5,)),
            dma((8,)),
            dma((4,)),
            dma((4,)),
            dma((groups - 1,)),
            dma((groups - 1,)),
            dma((xs - 1,)),
            dma((xs - 1,)),
            dma((xs - 1,)),
            dma((xs - 1,)),
            dma((zs - 1,)),
            dma((zs - 1,)),
            dma((zs - 1,)),
            dma((zs - 1,)),
        ],
        compiler_params=pltpu.CompilerParams(collective_id=0, has_side_effects=True),
    )(
        charges,
        jnp.swapaxes(leaf_basis, 1, 2),
        near_blocks,
        near_target.reshape(1, slots),
        near_source,
        near_count,
        leaf_far.T,
        leaf_far_couple.T,
        leaf_trans,
        dev_trans,
        dev_list,
        dev_couple,
        grp_couple,
        trans_leaf,
        trans_dev,
        jnp.transpose(couple_table, (1, 2, 0)),
    )


def solution(mesh):
    groups, per_group = mesh.shape["grp"], mesh.shape["dev"]
    xs = 4 if per_group % 4 == 0 and per_group > 4 else 2
    both = ("grp", "dev")
    return jax.shard_map(
        functools.partial(local, (groups, per_group // xs, xs)),
        mesh=mesh,
        in_specs=(
            P(both, None, None),
            P(both, None, None),
            P(both, None, None),
            P(both),
            P(both),
            P(both),
            P(both, None),
            P(both, None),
            P(both),
            P(both),
            P(both, None),
            P(both, None),
            P(),
            P(),
            P(),
            P(),
        ),
        out_specs=P(both, None, None),
        check_vma=False,
    )
```

```python
import functools

import jax
import jax.numpy as jnp
from jax import lax
from jax.experimental import pallas as pl
from jax.experimental.pallas import tpu as pltpu
from jax.sharding import PartitionSpec as P

f32, bf16 = jnp.float32, jnp.bfloat16
MESH = pl.DeviceIdType.MESH
TABLE_PITCH = 40
PROD_PITCH = 24
NEAR_PITCH = 40
U_MOM = 16
U_WIDE = 16
U_BOX = 16
U_TURN = 2
U_NEAR = 16
U_GATHER = 2
U_FAR = 4
U_FIN = 8
NT = (((1,), (1,)), ((), ()))


def split(x):
    high = x.astype(bf16)
    return high, (x - high.astype(f32)).astype(bf16)


def inside(index, size):
    return lax.min(lax.max(index, 0), size - 1)


def left_half(shape):
    return lax.broadcasted_iota(jnp.int32, shape, 1) < 64


def compact(doubled):
    high, low = split(doubled)
    return jnp.where(left_half(high.shape), high.astype(f32), low.astype(f32)).astype(bf16)


def doubled_sum(total):
    return total + pltpu.roll(total, 64, 1)


def spread_matrix():
    row = lax.broadcasted_iota(jnp.int32, (128, 512), 0)
    column = lax.broadcasted_iota(jnp.int32, (128, 512), 1)
    hit = (row >> 5 == column >> 7) & (row & 31 == column & 31)
    return hit.astype(f32).astype(bf16)


def spread(blocks, matrix):
    wide = jnp.dot(blocks, matrix, preferred_element_type=f32).astype(bf16)
    out = []
    for i in range(blocks.shape[0] // 16):
        rows = wide[i * 16 : (i + 1) * 16]
        out.append(jnp.concatenate([rows[:, g * 128 : (g + 1) * 128] for g in range(4)], axis=0))
    return out


def times_maps(wide, maps):
    weights = []
    for m in maps:
        weights.extend(split(m))
    weights = jnp.concatenate(weights, axis=0)
    if len(wide) == 1:
        lanes = wide[0][:, :64]
    else:
        half = left_half((64, 128))
        lanes = jnp.concatenate(
            [jnp.where(half, wide[i], wide[i + 1]) for i in range(0, len(wide), 2)], axis=1
        )
    return jnp.dot(lanes, weights, preferred_element_type=f32)


def fold(total):
    kept = jnp.where(
        left_half((16, 128)), total[0:16] + total[32:48], total[16:32] + total[48:64]
    )
    return doubled_sum(kept)


def kernel(
    sizes,
    charges,
    basis,
    blocks,
    target,
    source,
    count,
    far,
    far_couple,
    leaf_trans,
    dev_trans,
    dev_list,
    dev_couple,
    grp_couple,
    trans_leaf,
    trans_dev,
    couple,
    out,
    window,
    bt,
    blk,
    tl,
    td,
    raw,
    table,
    small,
    small_t,
    cwin,
    mwin,
    ubuf,
    xbuf,
    zbuf,
    bbuf,
    usend,
    vsend,
    wsend,
    prod,
    nbuf,
    farb,
    ybuf,
    local_sem,
    chunk_sem,
    halo_send,
    halo_recv,
    u_send,
    u_recv,
    x_send,
    x_recv,
    bx_send,
    bx_recv,
    z_send,
    z_recv,
    bz_send,
    bz_recv,
):
    groups, zs, xs = sizes
    per_group = zs * xs
    leaves = out.shape[0]
    margin = leaves // 2
    slots = blk.shape[0]
    types = table.shape[0]
    rows_of = table.reshape(types * TABLE_PITCH, 128)
    ntrans = tl.shape[0]
    chunks = 4
    per_chunk = 32 // chunks
    g, d = lax.axis_index("grp"), lax.axis_index("dev")
    z, x = lax.div(d, xs), lax.rem(d, xs)
    me = g * per_group + d
    total = groups * per_group
    right, left = lax.rem(me + 1, total), lax.rem(me + total - 1, total)
    first = me * leaves - margin

    def at(index):
        return {"grp": lax.div(index, per_group), "dev": lax.rem(index, per_group)}

    def group_peer(o):
        return {"grp": lax.rem(g + o, groups), "dev": d}

    def x_peer(o):
        return {"grp": g, "dev": z * xs + lax.rem(x + o, xs)}

    def z_peer(o):
        return {"grp": g, "dev": lax.rem(z + o, zs) * xs + x}

    loads = []
    for i, (a, b) in enumerate(
        (
            (charges, window.at[pl.ds(margin, leaves)]),
            (basis, bt),
            (trans_leaf, tl),
            (trans_dev, td),
        )
    ):
        loads.append(pltpu.make_async_copy(a, b, local_sem.at[i]))
    raw_loads = []
    for c in range(chunks):
        for half in range(2):
            rows = pl.ds(half * 32 + c * per_chunk, per_chunk)
            raw_loads.append(
                pltpu.make_async_copy(couple.at[rows], raw.at[rows], chunk_sem.at[c * 2 + half])
            )
    block_load = pltpu.make_async_copy(blocks, blk, local_sem.at[4])
    for copy in loads + raw_loads + [block_load]:
        copy.start()

    barrier = pltpu.get_barrier_semaphore()
    peers = (
        [at(left), at(right)]
        + [group_peer(o) for o in range(1, groups)]
        + [x_peer(o) for o in range(1, xs)]
        + [z_peer(o) for o in range(1, zs)]
    )
    for peer in peers:
        pl.semaphore_signal(barrier, inc=1, device_id=peer, device_id_type=MESH)

    matrix = spread_matrix()
    loads[2].wait()
    loads[3].wait()
    for i in range(2 * ntrans):
        m = tl[i] if i < ntrans else td[i - ntrans]
        small[i] = jnp.concatenate([m[:32], m[32:]], axis=1)
        small_t[i] = compact(jnp.concatenate([m, m], axis=1))

    loads[0].wait()
    loads[1].wait()

    def moments(step, carry):
        for j in range(U_MOM):
            leaf = step * U_MOM + j
            b = bt[leaf]
            m = lax.dot_general(
                window[margin + leaf],
                jnp.concatenate([b, b], axis=0),
                NT,
                preferred_element_type=f32,
            )
            cwin[margin + leaf] = compact(m)
        return carry

    lax.fori_loop(0, leaves // U_MOM, moments, 0)

    def widen(start):
        def body(step, carry):
            c = jnp.concatenate([cwin[start + step * U_WIDE + j] for j in range(U_WIDE)], axis=0)
            for j, w in enumerate(spread(c, matrix)):
                mwin[start + step * U_WIDE + j] = w
            return carry

        return body

    lax.fori_loop(0, leaves // U_WIDE, widen(margin), 0)

    def small_map(i):
        return small[i]

    def big_map(i):
        return table[i][:32]

    def to_box(step, carry):
        for i in range(0, U_BOX, 4):
            picks = [step * U_BOX + i + j for j in range(4)]
            carry = carry + times_maps(
                [mwin[margin + p] for p in picks], [small_map(leaf_trans[p]) for p in picks]
            )
        return carry

    box = compact(fold(lax.fori_loop(0, leaves // U_BOX, to_box, jnp.zeros((64, 128), f32))))
    bbuf[d] = box
    dtrans = dev_trans[0]
    usend[...] = compact(fold(times_maps(spread(box, matrix), [small_map(ntrans + dtrans)])))
    ubuf[g] = jnp.zeros((16, 128), bf16)

    pl.semaphore_wait(barrier, len(peers))

    def remote(src, dst, send, recv, i, peer):
        copy = pltpu.make_async_remote_copy(
            src_ref=src,
            dst_ref=dst,
            send_sem=send.at[i],
            recv_sem=recv.at[i],
            device_id=peer,
            device_id_type=MESH,
        )
        copy.start()
        return copy

    to_groups = [
        remote(usend, ubuf.at[g], u_send, u_recv, o - 1, group_peer(o)) for o in range(1, groups)
    ]
    box_x = [
        remote(bbuf.at[d], bbuf.at[d], bx_send, bx_recv, o - 1, x_peer(o))
        for o in range(1, xs)
    ]
    low, high = pl.ds(0, margin), pl.ds(leaves, margin)
    end_low, end_high = pl.ds(margin + leaves, margin), pl.ds(margin, margin)
    charge_halo = [
        remote(charges.at[pl.ds(leaves - margin, margin)], window.at[low], halo_send, halo_recv, 0, at(right)),
        remote(charges.at[pl.ds(0, margin)], window.at[end_low], halo_send, halo_recv, 1, at(left)),
    ]
    moment_halo = [
        remote(cwin.at[high], cwin.at[low], halo_send, halo_recv, 2, at(right)),
        remote(cwin.at[end_high], cwin.at[end_low], halo_send, halo_recv, 3, at(left)),
    ]

    for c in range(chunks):
        raw_loads[2 * c].wait()
        raw_loads[2 * c + 1].wait()

        def turn(i, carry):
            for j in range(U_TURN):
                k = c * per_chunk + i * U_TURN + j
                both = jnp.concatenate([raw[k], raw[k + 32]], axis=0)
                rows_of[pl.ds(k, types, stride=TABLE_PITCH), :] = both.T
            return carry

        lax.fori_loop(0, per_chunk // U_TURN, turn, 0)

    for copy in to_groups:
        copy.wait_recv()
    share = jnp.zeros((64, 128), f32)
    for h in range(0, groups, 4):
        picks = list(range(h, min(h + 4, groups)))
        rows = jnp.concatenate([ubuf[p] for p in picks], axis=0)
        share = share + times_maps(spread(rows, matrix), [big_map(grp_couple[g, p]) for p in picks])
    vsend[...] = compact(fold(share))
    xbuf[x] = vsend[...]
    share_x = [
        remote(vsend, xbuf.at[x], x_send, x_recv, o - 1, x_peer(o)) for o in range(1, xs)
    ]
    for copy in box_x:
        copy.wait_recv()
    plane = pl.ds(z * xs, xs)
    box_z = [
        remote(bbuf.at[plane], bbuf.at[plane], bz_send, bz_recv, o - 1, z_peer(o)) for o in range(1, zs)
    ]

    for copy in charge_halo:
        copy.wait_recv()
    block_load.wait()

    def near(step, carry):
        for j in range(U_NEAR):
            s = step * U_NEAR + j
            product = lax.dot_general(
                window[inside(source[s] - first, 2 * leaves)], blk[s], NT, preferred_element_type=f32
            )
            prod[pl.ds(pl.multiple_of(s * PROD_PITCH, 8), 16), :] = product
        return carry

    half_slots = slots // U_NEAR // 2
    lax.fori_loop(0, half_slots, near, 0)

    for copy in share_x:
        copy.wait_recv()
    row = xbuf[0].astype(f32)
    for i in range(1, xs):
        row = row + xbuf[i].astype(f32)
    wsend[...] = compact(doubled_sum(row))
    zbuf[z] = wsend[...]
    share_z = [
        remote(wsend, zbuf.at[z], z_send, z_recv, o - 1, z_peer(o)) for o in range(1, zs)
    ]

    lax.fori_loop(half_slots, slots // U_NEAR, near, 0)

    live = lax.broadcasted_iota(jnp.int32, (leaves, slots), 1) < count[0]
    which = lax.broadcasted_iota(jnp.int32, (leaves, slots), 0) + me * leaves
    pick = ((which == target[...]) & live).astype(f32).astype(bf16)

    def gather_near(step, carry):
        for i in range(U_GATHER):
            first_row = (step * U_GATHER + i) * 2
            rows = [prod[pl.ds(first_row + j, slots, stride=PROD_PITCH), :] for j in range(2)]
            high, low = split(jnp.concatenate(rows, axis=1))
            summed = jnp.dot(pick, high, preferred_element_type=f32) + jnp.dot(
                pick, low, preferred_element_type=f32
            )
            for j in range(2):
                start = pl.multiple_of((first_row + j) * NEAR_PITCH, 8)
                nbuf[pl.ds(start, leaves), :] = summed[:, j * 128 : (j + 1) * 128]
        return carry

    lax.fori_loop(0, 8 // U_GATHER, gather_near, 0)

    for copy in moment_halo:
        copy.wait_recv()
    lax.fori_loop(0, margin // U_WIDE, widen(0), 0)
    lax.fori_loop(0, margin // U_WIDE, widen(margin + leaves), 0)

    nfar = far.shape[0]

    def far_field(step, carry):
        for i in range(U_FAR):
            leaf = step * U_FAR + i
            acc = jnp.zeros((64, 128), f32)
            for f in range(0, nfar, 4):
                acc = acc + times_maps(
                    [mwin[inside(far[f + j, leaf] - first, 2 * leaves)] for j in range(4)],
                    [big_map(far_couple[f + j, leaf]) for j in range(4)],
                )
            farb[leaf] = fold(acc)[:, :64]
        return carry

    lax.fori_loop(0, leaves // U_FAR, far_field, 0)

    for copy in share_z:
        copy.wait_recv()
    for copy in box_z:
        copy.wait_recv()
    row = zbuf[0].astype(f32)
    for i in range(1, zs):
        row = row + zbuf[i].astype(f32)
    high_g, low_g = split(doubled_sum(row))
    down = lax.dot_general(
        jnp.concatenate([high_g, low_g], axis=0), small_t[ntrans + dtrans], NT, preferred_element_type=f32
    )
    listed = [inside(dev_list[0, n] - g * per_group, per_group) for n in range(4)]
    rows = jnp.concatenate([bbuf[b] for b in listed], axis=0)
    beside = fold(
        times_maps(spread(rows, matrix), [big_map(dev_couple[0, n]) for n in range(4)])
    )
    down = down[:16] + down[16:]
    high_b, low_b = split(jnp.concatenate([down, down], axis=1) + beside)
    both = jnp.concatenate([high_b, low_b], axis=0)
    for t in range(ntrans):
        y = lax.dot_general(both, small_t[t], NT, preferred_element_type=f32)
        ybuf[t] = y[:16] + y[16:]

    def finish(step, carry):
        for j in range(U_FIN):
            leaf = step * U_FIN + j
            rounded = (ybuf[leaf_trans[leaf]] + farb[leaf]).astype(bf16)
            out[leaf] = nbuf[pl.ds(leaf, 16, stride=NEAR_PITCH), :] + jnp.dot(
                rounded, bt[leaf], preferred_element_type=f32
            )
        return carry

    lax.fori_loop(0, leaves // U_FIN, finish, 0)

    for copy in to_groups + box_x + charge_halo + moment_halo + share_x + box_z + share_z:
        copy.wait_send()


def local(
    sizes,
    charges,
    leaf_basis,
    near_blocks,
    near_target,
    near_source,
    near_count,
    leaf_far,
    leaf_far_couple,
    leaf_trans,
    dev_trans,
    dev_list,
    dev_couple,
    grp_couple,
    trans_leaf,
    trans_dev,
    couple_table,
):
    groups, zs, xs = sizes
    leaves, r, panels = charges.shape
    slots = near_blocks.shape[0]
    types, k, _ = couple_table.shape
    ntrans = trans_leaf.shape[0]
    width = 2 * leaves
    hbm = pl.BlockSpec(memory_space=pl.ANY)
    smem = pl.BlockSpec(memory_space=pltpu.SMEM)
    vmem = pl.BlockSpec(memory_space=pltpu.VMEM)
    dma = pltpu.SemaphoreType.DMA
    return pl.pallas_call(
        functools.partial(kernel, sizes),
        out_shape=jax.ShapeDtypeStruct((leaves, r, panels), f32),
        in_specs=[hbm, hbm, hbm, vmem] + [smem] * 9 + [hbm, hbm, hbm],
        out_specs=vmem,
        scratch_shapes=[
            pltpu.VMEM((width, r, panels), bf16),
            pltpu.VMEM((leaves, k, panels), bf16),
            pltpu.VMEM((slots, panels, panels), bf16),
            pltpu.VMEM((ntrans, k, k), f32),
            pltpu.VMEM((ntrans, k, k), f32),
            pltpu.VMEM((k, k, types), f32),
            pltpu.VMEM((types, TABLE_PITCH, 128), f32),
            pltpu.VMEM((2 * ntrans, 32, 128), f32),
            pltpu.VMEM((2 * ntrans, k, 128), bf16),
            pltpu.VMEM((width, r, 128), bf16),
            pltpu.VMEM((width, 64, 128), bf16),
            pltpu.VMEM((groups, r, 128), bf16),
            pltpu.VMEM((xs, r, 128), bf16),
            pltpu.VMEM((zs, r, 128), bf16),
            pltpu.VMEM((zs * xs, r, 128), bf16),
            pltpu.VMEM((r, 128), bf16),
            pltpu.VMEM((r, 128), bf16),
            pltpu.VMEM((r, 128), bf16),
            pltpu.VMEM((slots * PROD_PITCH, panels), f32),
            pltpu.VMEM((r * NEAR_PITCH, panels), f32),
            pltpu.VMEM((leaves, r, k), f32),
            pltpu.VMEM((ntrans, r, k), f32),
            dma((5,)),
            dma((8,)),
            dma((4,)),
            dma((4,)),
            dma((groups - 1,)),
            dma((groups - 1,)),
            dma((xs - 1,)),
            dma((xs - 1,)),
            dma((xs - 1,)),
            dma((xs - 1,)),
            dma((zs - 1,)),
            dma((zs - 1,)),
            dma((zs - 1,)),
            dma((zs - 1,)),
        ],
        compiler_params=pltpu.CompilerParams(collective_id=0, has_side_effects=True),
    )(
        charges,
        jnp.swapaxes(leaf_basis, 1, 2),
        near_blocks,
        near_target.reshape(1, slots),
        near_source,
        near_count,
        leaf_far.T,
        leaf_far_couple.T,
        leaf_trans,
        dev_trans,
        dev_list,
        dev_couple,
        grp_couple,
        trans_leaf,
        trans_dev,
        jnp.transpose(couple_table, (1, 2, 0)),
    )


def solution(mesh):
    groups, per_group = mesh.shape["grp"], mesh.shape["dev"]
    xs = 4 if per_group % 4 == 0 and per_group > 4 else 2
    both = ("grp", "dev")
    return jax.shard_map(
        functools.partial(local, (groups, per_group // xs, xs)),
        mesh=mesh,
        in_specs=(
            P(both, None, None),
            P(both, None, None),
            P(both, None, None),
            P(both),
            P(both),
            P(both),
            P(both, None),
            P(both, None),
            P(both),
            P(both),
            P(both, None),
            P(both, None),
            P(),
            P(),
            P(),
            P(),
        ),
        out_specs=P(both, None, None),
        check_vma=False,
    )
```
